512 devices in a mesh: vocab: 64 (over x, y, core), hid: 8 (over z).
Axes of the slice: x: 4, y: 8, z: 8, core: 2. Of those that a mesh axis runs over, the one named last changes fastest.
Arguments:
- hidden_states: bfloat16 [768, 8192], P('vocab', 'hid'), may hold values from -10 to 10
- head_weight: bfloat16 [8192, 81920], P('hid', 'vocab'), may hold values from -8 to 8
- focus_tiles: int32 [4096, 2], P('vocab'), may hold values from 0 to 767, as said below
- focus_blocks: bfloat16 [4096, 128, 128], P('vocab'), may hold values from -0.5 to 0.5
Outputs:
- student_target: float32 [768, 98304], P('hid', 'vocab')
The draws below stay inside these ranges and needn't reach their ends.
Inputs may be any that keep to these rules, and one draw needn't show every extreme that they name: `focus_tiles`: rows k * 64 to (k + 1) * 64 - 1 name teacher tiles k * 10 to (k + 1) * 10 - 1 in column 0; column 1 is a student tile, whose owner is the tile divided by 12. Within each such block of rows no owner is named more than 2 times, and one owner, drawn from the seed, is named exactly 2 times in every block; other owners may be named 2 times as well.
All inputs are finite; a program needn't handle non-finite values.
Results may differ from the reference program's by a relative error of at most 0.0035.
Values may be sent and summed in bfloat16 or wider, within the bound.
A program may use at most 64 MiB of HBM per device.

```python
import math
import jax
import jax.numpy as jnp
from jax import lax

D = 8192
TILE = 128
TILES_DEV = 10
STILES_DEV = 12
CAP = 2
P_SIZE = 768
NNZ_DEV = 64
V = 81920
S = 98304
NNZ = 4096


def draw_hidden_states(key, part):
    noise_part = jnp.clip(jax.random.normal(jax.random.fold_in(key, 11), (P_SIZE, D), jnp.float32), -3.0, 3.0)
    row_scale = jnp.exp(jax.random.uniform(jax.random.fold_in(key, 29), (P_SIZE, 1), jnp.float32, math.log(0.1), 0.0))
    return (noise_part * row_scale).astype(jnp.bfloat16)


def draw_head_weight(key, part):
    noise_part = 3.0 / math.sqrt(D) * jnp.clip(jax.random.normal(jax.random.fold_in(key, 13), (D, V), jnp.float32), -4.0, 4.0)
    return noise_part.astype(jnp.bfloat16)


def draw_focus_tiles(key, part):
    senders = NNZ // NNZ_DEV
    hot_key, perm_key, teacher_key, student_key = jax.random.split(key, 4)
    hottest = jax.random.randint(hot_key, (), 0, senders)
    other_count = NNZ_DEV - CAP
    half_count = (other_count + 1) // 2

    def one_sender(sub_key):
        shuffle_key = jax.random.fold_in(sub_key, 101)
        chosen = jax.random.permutation(jax.random.fold_in(sub_key, 3), senders - 1)[:half_count]
        others = jnp.concatenate([chosen, chosen])[:other_count]
        others = others + (others >= hottest).astype(jnp.int32)
        owners = jnp.concatenate([jnp.full((CAP,), hottest, jnp.int32), others.astype(jnp.int32)])
        return owners[jax.random.permutation(shuffle_key, NNZ_DEV)]
    owners = jax.vmap(one_sender)(jax.random.split(perm_key, senders))
    sender_index = jnp.arange(senders, dtype=jnp.int32)[:, None]
    teacher = jax.random.randint(teacher_key, (senders, NNZ_DEV), 0, TILES_DEV) + sender_index * TILES_DEV
    student = owners * STILES_DEV + jax.random.randint(student_key, (senders, NNZ_DEV), 0, STILES_DEV)
    return jnp.stack([teacher, student], axis=-1).reshape(NNZ, 2).astype(jnp.int32)


def level_of(stream_key, extent, pieces, low, high):
    loudness = 1.0
    for dim, shards_of in pieces:
        steps = jax.random.uniform(jax.random.fold_in(jax.random.fold_in(stream_key, 6), dim), (shards_of,), jnp.float32, low / len(pieces), high / len(pieces))
        loudness = loudness * jnp.repeat(jnp.exp(steps), extent[dim] // shards_of).reshape((-1,) + (1,) * (len(extent) - 1 - dim))
    return loudness


def centred(stream_key, shape, width, limit, cuts=(), held_as=jnp.bfloat16):
    level = level_of(stream_key, shape, cuts, -0.22, 0.18) if cuts else 1.0
    array = jax.random.normal(stream_key, shape, jnp.float32) * width * level
    return jnp.minimum(jnp.maximum(array, -limit), limit).astype(held_as)


def setup_inputs(seed: int = 0) -> dict:
    keys = jax.random.split(jax.random.key(seed), 5)
    hidden_states = draw_hidden_states(jax.random.fold_in(keys[4], 71), 0)
    head_weight = draw_head_weight(jax.random.fold_in(keys[4], 71), 0)
    focus_tiles = draw_focus_tiles(jax.random.fold_in(keys[4], 71), 0)
    focus_blocks = centred(keys[3], (NNZ, TILE, TILE), TILE ** -0.5, 0.5, ((0, 64),))
    return {"hidden_states": hidden_states, "head_weight": head_weight, "focus_tiles": focus_tiles, "focus_blocks": focus_blocks}


def reference(hidden_states, head_weight, focus_tiles, focus_blocks):
    logits = jnp.dot(hidden_states, head_weight, preferred_element_type=jnp.float32)
    row_top = jnp.max(logits, axis=1, keepdims=True)
    exp_values = jnp.exp(logits - row_top)
    row_sum = jnp.sum(exp_values, axis=1, keepdims=True)
    weights = exp_values.astype(jnp.bfloat16)
    row_count = weights.shape[0]
    prob_tiles = weights.reshape(row_count, V // TILE, TILE)

    def add_entry(accumulator, entry_pair):
        coordinate, focus_block = entry_pair
        prob_tile = lax.dynamic_index_in_dim(prob_tiles, coordinate[0].astype(jnp.int32), 1, keepdims=False)
        term_rows = jnp.dot(prob_tile, focus_block, preferred_element_type=jnp.float32)
        previous = lax.dynamic_index_in_dim(accumulator, coordinate[1].astype(jnp.int32), 1, keepdims=False)
        accumulator = lax.dynamic_update_index_in_dim(accumulator, previous + term_rows, coordinate[1].astype(jnp.int32), 1)
        return accumulator, None

    accumulator = jnp.zeros((row_count, S // TILE, TILE), jnp.float32)
    accumulator, _ = lax.scan(add_entry, accumulator, (focus_tiles, focus_blocks))
    mapped = accumulator.reshape(row_count, S)
    return S * mapped / row_sum
```

```python
import functools

import jax
import jax.numpy as jnp
from jax import lax
from jax.experimental import pallas as pl
from jax.experimental.pallas import tpu as pltpu
from jax.sharding import PartitionSpec as P

TILE = 128
STILES = 12
CAP = 2
NX, NY, NC, NZ = 4, 8, 2, 8
MESH = pl.DeviceIdType.MESH
VMEM_LIMIT = 60 * 1024 * 1024
ORDER = (4, 3, -3, 2, -2, 1, -1, 0)
F32, BF16, I16, I32 = jnp.float32, jnp.bfloat16, jnp.int16, jnp.int32
TINY = 1e-30
FULL = 32767.0


def index_of(x, y, c):
    return (x * NY + y) * NC + c


def my_place():
    v = lax.axis_index("vocab")
    return v // (NY * NC), (v // NC) % NY, v % NC


def to_vocab(x, y, c):
    return {"vocab": index_of(x, y, c)}


def signal_all(peers):
    barrier = pltpu.get_barrier_semaphore()
    for peer in peers:
        pl.semaphore_signal(barrier, inc=1, device_id=peer, device_id_type=MESH)
    pl.semaphore_wait(barrier, len(peers))


def remote(src, dst, send_sem, recv_sem, peer):
    return pltpu.make_async_remote_copy(
        src_ref=src, dst_ref=dst, send_sem=send_sem, recv_sem=recv_sem,
        device_id=peer, device_id_type=MESH,
    )


def coded(value):
    top = jnp.maximum(jnp.max(jnp.abs(value), axis=1, keepdims=True), TINY)
    codes = jnp.round(value * (FULL / top)).astype(I32).astype(I16)
    return codes, top * (1.0 / FULL)


def lane_is(shape, lane):
    return lax.broadcasted_iota(I32, shape, 1) == lane


def ring_halves(step, side):
    if step == 0:
        return (0,) if side == 0 else (1,)
    return (0, 1)


def gather_logits_kernel(
    hid_ref, w_hbm, out_ref, w_ref, all_ref, part_ref,
    out_code, in_code, out_scale, in_scale,
    w_sem, own_sem, ysend, yrecv, xsend, xrecv, rsend, rrecv, csend, crecv,
    zsend, zrecv, zssend, zsrecv,
):
    x, y, c = my_place()
    z = lax.axis_index("hid")
    load_w = pltpu.make_async_copy(w_hbm, w_ref, w_sem)
    load_w.start()
    xs = ((x + 1) % NX, (x + NX - 1) % NX)
    zs = ((z + 1) % NZ, (z + NZ - 1) % NZ)
    peers = [to_vocab(x, (y + d) % NY, c) for d in range(1, NY)]
    peers += [to_vocab(n, y, c) for n in xs] + [to_vocab(x, y, 1 - c)]
    peers += [{"hid": n} for n in zs]
    signal_all(peers)

    me = index_of(x, y, c)
    sent = []
    arrived = {}

    def send(src, block, send_sem, recv_sem, peer):
        copy = remote(src, all_ref.at[block], send_sem, recv_sem, peer)
        copy.start()
        sent.append(copy)
        return copy

    for d in (4, 3, 5, 2, 6, 1, 7):
        arrived["y", d] = send(
            hid_ref, me, ysend.at[d], yrecv.at[d], to_vocab(x, (y + d) % NY, c)
        )
    own = pltpu.make_async_copy(hid_ref, all_ref.at[me], own_sem)
    own.start()
    for d in (0, 1, 7, 2, 6, 3, 5, 4):
        block = index_of(x, (y + NY - d) % NY, c)
        src = all_ref.at[block]
        if d == 0:
            src = hid_ref
        else:
            arrived["y", d].wait_recv()
        for side in (0, 1):
            arrived["x", side, d] = send(
                src, block, xsend.at[side, d], xrecv.at[side, d], to_vocab(xs[side], y, c)
            )
        arrived["c", 0, d] = send(
            src, block, csend.at[0, d], crecv.at[0, d], to_vocab(x, y, 1 - c)
        )
    for d in (0, 1, 7, 2, 6, 3, 5, 4):
        for side in (0, 1):
            arrived["x", side, d].wait_recv()
            block = index_of(xs[1 - side], (y + NY - d) % NY, c)
            src = all_ref.at[block]
            if d % 2 == side:
                arrived["r", d] = send(
                    src, block, rsend.at[d], rrecv.at[d], to_vocab(xs[side], y, c)
                )
            arrived["c", 1 + side, d] = send(
                src, block, csend.at[1 + side, d], crecv.at[1 + side, d],
                to_vocab(x, y, 1 - c),
            )
    for d in (0, 1, 7, 2, 6, 3, 5, 4):
        arrived["r", d].wait_recv()
        block = index_of((x + 2) % NX, (y + NY - d) % NY, c)
        arrived["c", 3, d] = send(
            all_ref.at[block], block, csend.at[3, d], crecv.at[3, d],
            to_vocab(x, y, 1 - c),
        )
    own.wait()
    load_w.wait()
    for kind in range(4):
        for d in range(NY):
            arrived["c", kind, d].wait_recv()

    columns = 256

    def partial(k):
        target = (z + ORDER[k] + NZ) % NZ
        rows = all_ref[pl.ds(target * 8, 8)].reshape(128, all_ref.shape[2])

        def body(n, carry):
            at = pl.ds(pl.multiple_of(n * columns, columns), columns)
            p = jnp.dot(rows, w_ref[:, at], preferred_element_type=F32)
            for i in range(4):
                q = p[32 * i : 32 * i + 32]
                part_ref[k, pl.ds(24 * i, 8), at] = q[0:8]
                part_ref[k, pl.ds(24 * i + 8, 8), at] = q[16:24]
                part_ref[k, pl.ds(24 * i + 16, 8), at] = q[8:16] + pltpu.roll(q[24:32], 4, 0)
            return carry

        lax.fori_loop(0, w_ref.shape[1] // columns, body, 0)

    def decoded(side, step, half, g):
        scale = in_scale[side, step, half][:, g : g + 1]
        return in_code[side, step, half, pl.ds(16 * g, 16), :].astype(F32) * scale

    hops = {}

    def wait_hop(side, step, half):
        for copy in hops[side, step, half]:
            copy.wait_recv()

    def hop(side, step, half, k):
        has_input = step >= 1 and half in ring_halves(step - 1, side)
        if has_input:
            wait_hop(side, step - 1, half)
        scales = jnp.zeros((16, 128), F32)
        for g in range(3):
            value = part_ref[k, pl.ds(48 * half + 16 * g, 16), :]
            if has_input:
                value = value + decoded(side, step - 1, half, g)
            codes, scale = coded(value)
            out_code[side, step, half, pl.ds(16 * g, 16), :] = codes
            scales = jnp.where(lane_is((16, 128), g), scale, scales)
        out_scale[side, step, half] = scales
        peer = {"hid": zs[side]}
        copies = (
            remote(out_scale.at[side, step, half], in_scale.at[side, step, half],
                   zssend.at[side, step, half], zsrecv.at[side, step, half], peer),
            remote(out_code.at[side, step, half], in_code.at[side, step, half],
                   zsend.at[side, step, half], zrecv.at[side, step, half], peer),
        )
        for copy in copies:
            copy.start()
            sent.append(copy)
        hops[side, step, half] = copies

    partial(0)
    for step in range(4):
        for half in (0, 1):
            for side in (0, 1):
                if half in ring_halves(step, side):
                    hop(side, step, half, 0 if step == 0 else 2 * step - 1 + side)
        if step < 3:
            partial(2 * step + 1)
            partial(2 * step + 2)
    partial(7)
    for half in (0, 1):
        for side in (0, 1):
            wait_hop(side, 3, half)
        for g in range(3):
            at = pl.ds(48 * half + 16 * g, 16)
            out_ref[at, :] = (
                part_ref[7, at, :] + decoded(0, 3, half, g) + decoded(1, 3, half, g)
            )
    for copy in sent:
        copy.wait_send()


def gather_logits(hidden, head_weight):
    depth, width = head_weight.shape
    dma = pltpu.SemaphoreType.DMA
    return pl.pallas_call(
        gather_logits_kernel,
        out_shape=jax.ShapeDtypeStruct((96, width), F32),
        in_specs=[
            pl.BlockSpec(memory_space=pltpu.VMEM),
            pl.BlockSpec(memory_space=pl.ANY),
        ],
        out_specs=pl.BlockSpec(memory_space=pltpu.VMEM),
        scratch_shapes=[
            pltpu.VMEM((depth, width), BF16),
            pltpu.VMEM((NX * NY * NC, 16, depth), BF16),
            pltpu.VMEM((8, 96, width), F32),
            pltpu.VMEM((2, 4, 2, 48, width), I16),
            pltpu.VMEM((2, 4, 2, 48, width), I16),
            pltpu.VMEM((2, 4, 2, 16, 128), F32),
            pltpu.VMEM((2, 4, 2, 16, 128), F32),
            dma, dma, dma((NY,)), dma((NY,)), dma((2, NY)), dma((2, NY)),
            dma((NY,)), dma((NY,)), dma((4, NY)), dma((4, NY)),
            dma((2, 4, 2)), dma((2, 4, 2)), dma((2, 4, 2)), dma((2, 4, 2)),
        ],
        compiler_params=pltpu.CompilerParams(
            collective_id=0, has_side_effects=True, vmem_limit_bytes=VMEM_LIMIT
        ),
        name="gather_logits",
    )(hidden, head_weight)


def map_tiles_kernel(tiles_ref, logits_ref, blocks_ref, slots_ref, meta_ref, weights_ref, count_ref):
    teacher_tiles = logits_ref.shape[1] // TILE
    first = lax.axis_index("vocab") * teacher_tiles
    stats = jnp.zeros((6, 16, 128), F32)
    pieces = []
    for g in range(6):
        rows = pl.ds(16 * g, 16)
        logits = logits_ref[rows, :]
        top = jnp.max(logits, axis=1, keepdims=True)
        values = jnp.exp(logits - top)
        total = jnp.sum(values, axis=1, keepdims=True)
        for t in range(teacher_tiles):
            weights_ref[t, rows, :] = values[:, t * TILE : (t + 1) * TILE].astype(BF16)
        pieces.append((top, total))
    stats = jnp.zeros((16, 128), F32)
    for g, (top, total) in enumerate(pieces):
        stats = jnp.where(lane_is((16, 128), g), top, stats)
        stats = jnp.where(lane_is((16, 128), 8 + g), total, stats)
    for d in range(8):
        meta_ref[d, 0:16, :] = jnp.full((16, 128), -1.0, F32)
        meta_ref[d, 16:32, :] = stats

    def clear(i, carry):
        slots_ref[i] = jnp.zeros((96, TILE), BF16)
        return carry

    lax.fori_loop(0, slots_ref.shape[0], clear, 0)

    def clear_count(i, carry):
        count_ref[i] = 0
        return carry

    lax.fori_loop(0, count_ref.shape[0], clear_count, 0)

    def entry(e, carry):
        student = tiles_ref[e, 1]
        owner = student // STILES
        label = student - owner * STILES
        rank = count_ref[owner]
        count_ref[owner] = rank + 1
        group = (owner // (NY * NC)) * NC + owner % NC
        line = ((owner // NC) % NY) * CAP + rank
        product = jnp.dot(
            weights_ref[tiles_ref[e, 0] - first], blocks_ref[e], preferred_element_type=F32
        )
        slots_ref[group * (NY * CAP) + line] = product.astype(BF16)
        meta_ref[group, pl.ds(line, 1), :] = jnp.full((1, 128), label.astype(F32))
        return carry

    lax.fori_loop(0, tiles_ref.shape[0], entry, 0, unroll=4)


def map_tiles(focus_tiles, logits, focus_blocks):
    groups = NX * NC
    return pl.pallas_call(
        map_tiles_kernel,
        out_shape=(
            jax.ShapeDtypeStruct((groups * NY * CAP, 96, TILE), BF16),
            jax.ShapeDtypeStruct((groups, 32, 128), F32),
        ),
        in_specs=[
            pl.BlockSpec(memory_space=pltpu.SMEM),
            pl.BlockSpec(memory_space=pltpu.VMEM),
            pl.BlockSpec(memory_space=pltpu.VMEM),
        ],
        out_specs=(
            pl.BlockSpec(memory_space=pltpu.VMEM),
            pl.BlockSpec(memory_space=pltpu.VMEM),
        ),
        scratch_shapes=[
            pltpu.VMEM((logits.shape[1] // TILE, 96, TILE), BF16),
            pltpu.SMEM((NX * NY * NC,), I32),
        ],
        compiler_params=pltpu.CompilerParams(vmem_limit_bytes=VMEM_LIMIT),
        name="map_tiles",
    )(focus_tiles, logits, focus_blocks)


def exchange_kernel(
    slots_hbm, meta_hbm, out_ref, slots_in, meta_in, factor_ref, group_ref, done_ref,
    out_code, in_code, out_stat, in_stat,
    ssend, srecv, msend, mrecv, ysend, yrecv, tsend, trecv,
):
    x, y, c = my_place()
    width = STILES * TILE
    ys = ((y + 1) % NY, (y + NY - 1) % NY)

    def place(o):
        return (x + o // 2) % NX, (c + o % 2) % NC

    peers = []
    for o in range(1, 8):
        px, pc = place(o)
        peers.append(to_vocab(px, y, pc))
    peers += [to_vocab(x, n, c) for n in ys]
    signal_all(peers)

    sent = []
    came = {}
    for o in range(8):
        px, pc = place(o)
        src = meta_hbm.at[px * NC + pc]
        if o == 0:
            copy = pltpu.make_async_copy(src, meta_in.at[0], mrecv.at[0])
        else:
            copy = remote(src, meta_in.at[o], msend.at[o], mrecv.at[o], to_vocab(px, y, pc))
            sent.append(copy)
        copy.start()
        came["m", o] = copy
    for k in range(8):
        row = (y + ORDER[k] + NY) % NY
        for o in (4, 5, 2, 6, 3, 7, 1, 0):
            px, pc = place(o)
            src = slots_hbm.at[pl.ds(((px * NC + pc) * NY + row) * CAP, CAP)]
            if o == 0:
                copy = pltpu.make_async_copy(src, slots_in.at[k, 0], srecv.at[k, 0])
            else:
                copy = remote(
                    src, slots_in.at[k, o], ssend.at[k, o], srecv.at[k, o],
                    to_vocab(px, y, pc),
                )
                sent.append(copy)
            copy.start()
            came[k, o] = copy

    def wait_came(key):
        if key[1] == 0:
            came[key].wait()
        else:
            came[key].wait_recv()

    for o in range(8):
        wait_came(("m", o))
    groups = jnp.zeros((16, 128), F32)
    for g in range(6):
        tops = [meta_in[o, 16:32, g : g + 1] for o in range(8)]
        top = functools.reduce(jnp.maximum, tops)
        total = jnp.zeros((16, 1), F32)
        for o in range(8):
            factor = jnp.exp(tops[o] - top)
            total = total + factor * meta_in[o, 16:32, 8 + g : 9 + g]
            factor_ref[o, pl.ds(16 * g, 16), :] = jnp.broadcast_to(factor, (16, 128))
        groups = jnp.where(lane_is((16, 128), g), top, groups)
        groups = jnp.where(lane_is((16, 128), 8 + g), total, groups)
    group_ref[...] = groups

    def merged(k, at):
        row = (y + ORDER[k] + NY) % NY
        tiles = [jnp.zeros((16, TILE), F32)] * STILES
        for o in range(8):
            factor = factor_ref[o, at, :]
            for i in range(CAP):
                tile = slots_in[k, o, i, at, :].astype(F32) * factor
                label = meta_in[o, pl.ds(row * CAP + i, 1), :]
                for j in range(STILES):
                    tiles[j] = tiles[j] + jnp.where(label == float(j), tile, 0.0)
        return tiles

    hops = {}

    def wait_hop(side, step, half):
        for copy in hops[side, step, half]:
            copy.wait_recv()

    def incoming(side, step, half, g):
        stat = in_stat[side, step, half]
        return stat[:, g : g + 1], stat[:, 8 + g : 9 + g], stat[:, 16 + g : 17 + g]

    def hop(side, step, half, k):
        has_input = step >= 1 and half in ring_halves(step - 1, side)
        if has_input:
            wait_hop(side, step - 1, half)
        stats = jnp.zeros((16, 128), F32)
        for g in range(3):
            row_at = pl.ds(48 * half + 16 * g, 16)
            code_at = pl.ds(16 * g, 16)
            tiles = merged(k, row_at)
            lane = 3 * half + g
            top = group_ref[:, lane : lane + 1]
            total = group_ref[:, 8 + lane : 9 + lane]
            if has_input:
                scale, in_top, in_total = incoming(side, step - 1, half, g)
                new_top = jnp.maximum(top, in_top)
                mine = jnp.exp(top - new_top)
                theirs = jnp.exp(in_top - new_top)
                total = total * mine + in_total * theirs
                scale = scale * theirs
                top = new_top
                for j in range(STILES):
                    code = in_code[side, step - 1, half, code_at, j * TILE : (j + 1) * TILE]
                    tiles[j] = tiles[j] * mine + code.astype(F32) * scale
            codes, scale = coded(jnp.concatenate(tiles, axis=1))
            out_code[side, step, half, code_at, :] = codes
            stats = jnp.where(lane_is((16, 128), g), scale, stats)
            stats = jnp.where(lane_is((16, 128), 8 + g), top, stats)
            stats = jnp.where(lane_is((16, 128), 16 + g), total, stats)
        out_stat[side, step, half] = stats
        peer = to_vocab(x, ys[side], c)
        copies = (
            remote(out_stat.at[side, step, half], in_stat.at[side, step, half],
                   tsend.at[side, step, half], trecv.at[side, step, half], peer),
            remote(out_code.at[side, step, half], in_code.at[side, step, half],
                   ysend.at[side, step, half], yrecv.at[side, step, half], peer),
        )
        for copy in copies:
            copy.start()
            sent.append(copy)
        hops[side, step, half] = copies

    def wait_stage(k):
        for o in range(8):
            wait_came((k, o))

    for step in range(4):
        if step == 0:
            wait_stage(0)
            hop(0, 0, 0, 0)
            hop(1, 0, 1, 0)
        else:
            for side in (0, 1):
                k = 2 * step - 1 + side
                wait_stage(k)
                fresh = 1 if side == 0 else 0
                order = (fresh, 1 - fresh) if step == 1 else (0, 1)
                for half in order:
                    hop(side, step, half, k)
    wait_stage(7)
    for half in (0, 1):
        for side in (0, 1):
            wait_hop(side, 3, half)
        for g in range(3):
            row_at = pl.ds(48 * half + 16 * g, 16)
            code_at = pl.ds(16 * g, 16)
            tiles = merged(7, row_at)
            lane = 3 * half + g
            top = group_ref[:, lane : lane + 1]
            total = group_ref[:, 8 + lane : 9 + lane]
            parts = [incoming(side, 3, half, g) for side in (0, 1)]
            new_top = jnp.maximum(top, jnp.maximum(parts[0][1], parts[1][1]))
            mine = jnp.exp(top - new_top)
            theirs = [jnp.exp(part[1] - new_top) for part in parts]
            total = total * mine + parts[0][2] * theirs[0] + parts[1][2] * theirs[1]
            share = float(width * NX * NY * NC) / total
            for j in range(STILES):
                cols = slice(j * TILE, (j + 1) * TILE)
                value = tiles[j] * mine
                for side in (0, 1):
                    code = in_code[side, 3, half, code_at, cols]
                    value = value + code.astype(F32) * (parts[side][0] * theirs[side])
                done_ref[row_at, cols] = value * share
    early = lax.broadcasted_iota(I32, (8, width), 0) < 4
    for p in range(4):
        second = pltpu.roll(done_ref[24 * p + 8 : 24 * p + 16, :], 4, 0)
        mixed = done_ref[24 * p + 16 : 24 * p + 24, :]
        out_ref[24 * p : 24 * p + 8, :] = done_ref[24 * p : 24 * p + 8, :]
        out_ref[24 * p + 8 : 24 * p + 16, :] = jnp.where(early, mixed, second)
        out_ref[24 * p + 16 : 24 * p + 24, :] = jnp.where(early, second, mixed)
    for copy in sent:
        copy.wait_send()


def exchange(slots, meta):
    width = STILES * TILE
    dma = pltpu.SemaphoreType.DMA
    return pl.pallas_call(
        exchange_kernel,
        out_shape=jax.ShapeDtypeStruct((96, width), F32),
        in_specs=[pl.BlockSpec(memory_space=pl.ANY)] * 2,
        out_specs=pl.BlockSpec(memory_space=pltpu.VMEM),
        scratch_shapes=[
            pltpu.VMEM((8, 8, CAP, 96, TILE), BF16),
            pltpu.VMEM((8, 32, 128), F32),
            pltpu.VMEM((8, 96, TILE), F32),
            pltpu.VMEM((16, 128), F32),
            pltpu.VMEM((96, width), F32),
            pltpu.VMEM((2, 4, 2, 48, width), I16),
            pltpu.VMEM((2, 4, 2, 48, width), I16),
            pltpu.VMEM((2, 4, 2, 16, 128), F32),
            pltpu.VMEM((2, 4, 2, 16, 128), F32),
            dma((8, 8)), dma((8, 8)), dma((8,)), dma((8,)),
            dma((2, 4, 2)), dma((2, 4, 2)), dma((2, 4, 2)), dma((2, 4, 2)),
        ],
        compiler_params=pltpu.CompilerParams(
            collective_id=1, has_side_effects=True, vmem_limit_bytes=VMEM_LIMIT
        ),
        name="exchange",
    )(slots, meta)


def per_device(hidden_states, head_weight, focus_tiles, focus_blocks):
    hidden = jnp.pad(hidden_states, ((0, 16 - hidden_states.shape[0]), (0, 0)))
    logits = gather_logits(hidden, head_weight)
    slots, meta = map_tiles(focus_tiles, logits, focus_blocks)
    return exchange(slots, meta)


def solution(mesh):
    return jax.shard_map(
        per_device,
        mesh=mesh,
        in_specs=(P("vocab", "hid"), P("hid", "vocab"), P("vocab", None), P("vocab", None, None)),
        out_specs=P("hid", "vocab"),
        check_vma=False,
    )
```

```python
import functools

import jax
import jax.numpy as jnp
from jax import lax
from jax.experimental import pallas as pl
from jax.experimental.pallas import tpu as pltpu
from jax.sharding import PartitionSpec as P

TILE = 128
STILES = 12
CAP = 2
TEACHER_TILES = 10
NX, NY, NC, NZ = 4, 8, 2, 8
MESH = pl.DeviceIdType.MESH
VMEM_LIMIT = 60 * 1024 * 1024
ORDER = (4, 3, -3, 2, -2, 1, -1, 0)
F32, BF16, I16, I32 = jnp.float32, jnp.bfloat16, jnp.int16, jnp.int32
TINY = 1e-30
FULL = 32767.0


def index_of(x, y, c):
    return (x * NY + y) * NC + c


def my_place():
    v = lax.axis_index("vocab")
    return v // (NY * NC), (v // NC) % NY, v % NC


def to_vocab(x, y, c):
    return {"vocab": index_of(x, y, c)}


def signal_all(peers):
    barrier = pltpu.get_barrier_semaphore()
    for peer in peers:
        pl.semaphore_signal(barrier, inc=1, device_id=peer, device_id_type=MESH)
    pl.semaphore_wait(barrier, len(peers))


def remote(src, dst, send_sem, recv_sem, peer):
    return pltpu.make_async_remote_copy(
        src_ref=src, dst_ref=dst, send_sem=send_sem, recv_sem=recv_sem,
        device_id=peer, device_id_type=MESH,
    )


def coded(value):
    top = jnp.maximum(jnp.max(jnp.abs(value), axis=1, keepdims=True), TINY)
    codes = jnp.round(value * (FULL / top)).astype(I32).astype(I16)
    return codes, top * (1.0 / FULL)


def lane_is(shape, lane):
    return lax.broadcasted_iota(I32, shape, 1) == lane


def ring_halves(step, side):
    return ((side,), (1 - side, side), (0, 1), (0, 1))[step]


def plan_kernel(tiles_ref, entry_ref, teacher_ref, valid_ref, label_ref, count_ref):
    first = lax.axis_index("vocab") * TEACHER_TILES
    label_ref[...] = jnp.full(label_ref.shape, -1.0, F32)

    def clear(i, carry):
        entry_ref[i] = 0
        teacher_ref[i] = 0
        valid_ref[i] = 0.0
        return carry

    lax.fori_loop(0, NX * NY * NC * CAP, clear, 0, unroll=8)

    def clear_count(i, carry):
        count_ref[i] = 0
        return carry

    lax.fori_loop(0, NX * NY * NC, clear_count, 0, unroll=8)

    def entry(e, carry):
        student = tiles_ref[e, 1]
        owner = student // STILES
        label = student - owner * STILES
        rank = count_ref[owner]
        count_ref[owner] = rank + 1
        group = (owner // (NY * NC)) * NC + owner % NC
        line = ((owner // NC) % NY) * CAP + rank
        slot = group * (NY * CAP) + line
        entry_ref[slot] = e
        teacher_ref[slot] = tiles_ref[e, 0] - first
        valid_ref[slot] = 1.0
        label_ref[group, pl.ds(line, 1), :] = jnp.full((1, 128), label.astype(F32))
        return carry

    lax.fori_loop(0, tiles_ref.shape[0], entry, 0, unroll=4)


def plan(focus_tiles):
    slots = NX * NY * NC * CAP
    smem = pl.BlockSpec(memory_space=pltpu.SMEM)
    return pl.pallas_call(
        plan_kernel,
        out_shape=(
            jax.ShapeDtypeStruct((slots,), I32),
            jax.ShapeDtypeStruct((slots,), I32),
            jax.ShapeDtypeStruct((slots,), F32),
            jax.ShapeDtypeStruct((NX * NC, NY * CAP, 128), F32),
        ),
        in_specs=[smem],
        out_specs=(smem, smem, smem, pl.BlockSpec(memory_space=pltpu.VMEM)),
        scratch_shapes=[pltpu.SMEM((NX * NY * NC,), I32)],
        name="plan",
    )(focus_tiles)


def whole_kernel(
    entry_ref, teacher_ref, valid_ref, hid_ref, w_hbm, blocks_hbm, label_hbm, out_ref,
    w_ref, blocks_ref, all_ref, part_ref, zout, zin, zout_scale, zin_scale, logits_ref,
    weights_ref, slots_ref, slots_in, label_in, stat_ref, stat_in, factor_ref, group_ref,
    done_ref, yout, yin, yout_stat, yin_stat,
    w_sem, blocks_sem, own_sem, ysend, yrecv, xsend, xrecv, rsend, rrecv, csend, crecv,
    zsend, zrecv, zssend, zsrecv, ssend, srecv, lsend, lrecv, tsend, trecv,
    hsend, hrecv, hssend, hsrecv,
):
    x, y, c = my_place()
    z = lax.axis_index("hid")
    load_w = pltpu.make_async_copy(w_hbm, w_ref, w_sem)
    load_w.start()
    load_blocks = pltpu.make_async_copy(blocks_hbm, blocks_ref, blocks_sem)
    load_blocks.start()
    xs = ((x + 1) % NX, (x + NX - 1) % NX)
    ys = ((y + 1) % NY, (y + NY - 1) % NY)
    zs = ((z + 1) % NZ, (z + NZ - 1) % NZ)

    def place(o):
        return (x + o // 2) % NX, (c + o % 2) % NC

    def place_vocab(o):
        px, pc = place(o)
        return to_vocab(px, y, pc)

    peers = [to_vocab(x, (y + d) % NY, c) for d in range(1, NY)]
    peers += [place_vocab(o) for o in range(1, 8)]
    peers += [{"hid": n} for n in zs]
    signal_all(peers)

    me = index_of(x, y, c)
    sent = []
    arrived = {}

    def send(src, block, send_sem, recv_sem, peer):
        copy = remote(src, all_ref.at[block], send_sem, recv_sem, peer)
        copy.start()
        sent.append(copy)
        return copy

    for d in (4, 3, 5, 2, 6, 1, 7):
        arrived["y", d] = send(
            hid_ref, me, ysend.at[d], yrecv.at[d], to_vocab(x, (y + d) % NY, c)
        )
    own = pltpu.make_async_copy(hid_ref, all_ref.at[me], own_sem)
    own.start()
    for d in (0, 1, 7, 2, 6, 3, 5, 4):
        block = index_of(x, (y + NY - d) % NY, c)
        src = all_ref.at[block]
        if d == 0:
            src = hid_ref
        else:
            arrived["y", d].wait_recv()
        for side in (0, 1):
            arrived["x", side, d] = send(
                src, block, xsend.at[side, d], xrecv.at[side, d], to_vocab(xs[side], y, c)
            )
        arrived["c", 0, d] = send(
            src, block, csend.at[0, d], crecv.at[0, d], to_vocab(x, y, 1 - c)
        )
    for d in (0, 1, 7, 2, 6, 3, 5, 4):
        for side in (0, 1):
            arrived["x", side, d].wait_recv()
            block = index_of(xs[1 - side], (y + NY - d) % NY, c)
            src = all_ref.at[block]
            if d % 2 == side:
                arrived["r", d] = send(
                    src, block, rsend.at[d], rrecv.at[d], to_vocab(xs[side], y, c)
                )
            arrived["c", 1 + side, d] = send(
                src, block, csend.at[1 + side, d], crecv.at[1 + side, d],
                to_vocab(x, y, 1 - c),
            )
    for d in (0, 1, 7, 2, 6, 3, 5, 4):
        arrived["r", d].wait_recv()
        block = index_of((x + 2) % NX, (y + NY - d) % NY, c)
        arrived["c", 3, d] = send(
            all_ref.at[block], block, csend.at[3, d], crecv.at[3, d],
            to_vocab(x, y, 1 - c),
        )
    own.wait()
    load_w.wait()
    for kind in range(4):
        for d in range(NY):
            arrived["c", kind, d].wait_recv()

    came = {}
    for o in range(8):
        px, pc = place(o)
        src = label_hbm.at[px * NC + pc]
        if o == 0:
            copy = pltpu.make_async_copy(src, label_in.at[0], lrecv.at[0])
        else:
            copy = remote(src, label_in.at[o], lsend.at[o], lrecv.at[o], place_vocab(o))
            sent.append(copy)
        copy.start()
        came["l", o] = copy

    def wait_came(key):
        if key[-1] == 0:
            came[key].wait()
        else:
            came[key].wait_recv()

    columns = 256

    def partial(k):
        target = (z + ORDER[k] + NZ) % NZ
        rows = all_ref[pl.ds(target * 8, 8)].reshape(128, all_ref.shape[2])

        def body(n, carry):
            at = pl.ds(pl.multiple_of(n * columns, columns), columns)
            p = jnp.dot(rows, w_ref[:, at], preferred_element_type=F32)
            for i in range(4):
                q = p[32 * i : 32 * i + 32]
                part_ref[k, pl.ds(24 * i, 8), at] = q[0:8]
                part_ref[k, pl.ds(24 * i + 8, 8), at] = q[16:24]
                part_ref[k, pl.ds(24 * i + 16, 8), at] = q[8:16] + pltpu.roll(q[24:32], 4, 0)
            return carry

        lax.fori_loop(0, w_ref.shape[1] // columns, body, 0)

    zhalf = w_ref.shape[1] // 2
    hops = {}

    def send_hop(key, copies):
        for copy in copies:
            copy.start()
            sent.append(copy)
        hops[key] = copies

    def wait_hop(key):
        for copy in hops[key]:
            copy.wait_recv()

    def zvalue(at, g):
        return zin[at + (pl.ds(16 * g, 16),)].astype(F32) * zin_scale[at][:, g : g + 1]

    def zhop(part, side, step, ch, k):
        at = (part, side, step, ch)
        before = (part, side, step - 1, ch)
        has_input = step >= 1 and ch in ring_halves(step - 1, side)
        if has_input:
            wait_hop(("z",) + before)
        scales = jnp.zeros((16, 128), F32)
        for g in range(3):
            value = part_ref[k, pl.ds(48 * part + 16 * g, 16), ch * zhalf : (ch + 1) * zhalf]
            if has_input:
                value = value + zvalue(before, g)
            codes, scale = coded(value)
            zout[at + (pl.ds(16 * g, 16),)] = codes
            scales = jnp.where(lane_is((16, 128), g), scale, scales)
        zout_scale[at] = scales
        peer = {"hid": zs[side]}
        send_hop(("z",) + at, (
            remote(zout_scale.at[at], zin_scale.at[at], zssend.at[at], zsrecv.at[at], peer),
            remote(zout.at[at], zin.at[at], zsend.at[at], zrecv.at[at], peer),
        ))

    def zstep(part, step):
        for turn in (0, 1):
            for side in (0, 1):
                if turn < len(ring_halves(step, side)):
                    k = 0 if step == 0 else 2 * step - 1 + side
                    zhop(part, side, step, ring_halves(step, side)[turn], k)

    def zfinal(part):
        for ch in (0, 1):
            cols = slice(ch * zhalf, (ch + 1) * zhalf)
            for side in (0, 1):
                wait_hop(("z", part, side, 3, ch))
            for g in range(3):
                rows = pl.ds(48 * part + 16 * g, 16)
                logits_ref[rows, cols] = (
                    part_ref[7, rows, cols]
                    + zvalue((part, 0, 3, ch), g)
                    + zvalue((part, 1, 3, ch), g)
                )

    def map_and_send(part):
        stats = jnp.zeros((16, 128), F32)
        for g in range(3):
            logits = logits_ref[pl.ds(48 * part + 16 * g, 16), :]
            top = jnp.max(logits, axis=1, keepdims=True)
            values = jnp.exp(logits - top)
            total = jnp.sum(values, axis=1, keepdims=True)
            for t in range(TEACHER_TILES):
                weights_ref[part, t, pl.ds(16 * g, 16), :] = values[
                    :, t * TILE : (t + 1) * TILE
                ].astype(BF16)
            stats = jnp.where(lane_is((16, 128), g), top, stats)
            stats = jnp.where(lane_is((16, 128), 8 + g), total, stats)
        stat_ref[part] = stats
        for o in range(8):
            src, dst = stat_ref.at[part], stat_in.at[part, o]
            if o == 0:
                copy = pltpu.make_async_copy(src, dst, trecv.at[part, 0])
            else:
                copy = remote(src, dst, tsend.at[part, o], trecv.at[part, o], place_vocab(o))
                sent.append(copy)
            copy.start()
            came["t", part, o] = copy
        for k in range(8):
            row = (y + ORDER[k] + NY) % NY

            def products(o, carry, row=row):
                base = (((x + o // 2) % NX * NC + (c + o % 2) % NC) * NY + row) * CAP
                for i in range(CAP):
                    product = jnp.dot(
                        weights_ref[part, teacher_ref[base + i]],
                        blocks_ref[entry_ref[base + i]],
                        preferred_element_type=F32,
                    )
                    slots_ref[part, base + i] = (product * valid_ref[base + i]).astype(BF16)
                return carry

            lax.fori_loop(0, 8, products, 0, unroll=4)
            for o in (4, 5, 2, 6, 3, 7, 1, 0):
                px, pc = place(o)
                src = slots_ref.at[part, pl.ds(((px * NC + pc) * NY + row) * CAP, CAP)]
                at = (part, k, o)
                if o == 0:
                    copy = pltpu.make_async_copy(src, slots_in.at[at], srecv.at[at])
                else:
                    copy = remote(
                        src, slots_in.at[at], ssend.at[at], srecv.at[at], place_vocab(o)
                    )
                    sent.append(copy)
                copy.start()
                came[("s",) + at] = copy

    def factors(part):
        for o in range(8):
            wait_came(("t", part, o))
        groups = jnp.zeros((16, 128), F32)
        for g in range(3):
            tops = [stat_in[part, o, :, g : g + 1] for o in range(8)]
            top = functools.reduce(jnp.maximum, tops)
            total = jnp.zeros((16, 1), F32)
            for o in range(8):
                factor = jnp.exp(tops[o] - top)
                total = total + factor * stat_in[part, o, :, 8 + g : 9 + g]
                factor_ref[part, o, pl.ds(16 * g, 16), :] = jnp.broadcast_to(factor, (16, 128))
            groups = jnp.where(lane_is((16, 128), g), top, groups)
            groups = jnp.where(lane_is((16, 128), 8 + g), total, groups)
        group_ref[part] = groups

    half_tiles = STILES // 2

    def merged(part, k, g, ch):
        row = (y + ORDER[k] + NY) % NY
        at = pl.ds(16 * g, 16)
        tiles = [jnp.zeros((16, TILE), F32)] * half_tiles
        for o in range(8):
            factor = factor_ref[part, o, at, :]
            for i in range(CAP):
                tile = slots_in[part, k, o, i, at, :].astype(F32) * factor
                label = label_in[o, pl.ds(row * CAP + i, 1), :]
                for j in range(half_tiles):
                    mine = label == float(ch * half_tiles + j)
                    tiles[j] = tiles[j] + jnp.where(mine, tile, 0.0)
        group = group_ref[part]
        return tiles, group[:, g : g + 1], group[:, 8 + g : 9 + g]

    def incoming(at, g):
        stat = yin_stat[at]
        return stat[:, g : g + 1], stat[:, 8 + g : 9 + g], stat[:, 16 + g : 17 + g]

    def yhop(part, side, step, ch, k):
        at = (part, side, step, ch)
        before = (part, side, step - 1, ch)
        has_input = step >= 1 and ch in ring_halves(step - 1, side)
        if has_input:
            wait_hop(("y",) + before)
        stats = jnp.zeros((16, 128), F32)
        for g in range(3):
            tiles, top, total = merged(part, k, g, ch)
            if has_input:
                scale, in_top, in_total = incoming(before, g)
                new_top = jnp.maximum(top, in_top)
                mine = jnp.exp(top - new_top)
                theirs = jnp.exp(in_top - new_top)
                total = total * mine + in_total * theirs
                scale = scale * theirs
                top = new_top
                for j in range(half_tiles):
                    code = yin[before + (pl.ds(16 * g, 16), pl.ds(j * TILE, TILE))]
                    tiles[j] = tiles[j] * mine + code.astype(F32) * scale
            codes, scale = coded(jnp.concatenate(tiles, axis=1))
            yout[at + (pl.ds(16 * g, 16),)] = codes
            stats = jnp.where(lane_is((16, 128), g), scale, stats)
            stats = jnp.where(lane_is((16, 128), 8 + g), top, stats)
            stats = jnp.where(lane_is((16, 128), 16 + g), total, stats)
        yout_stat[at] = stats
        peer = to_vocab(x, ys[side], c)
        send_hop(("y",) + at, (
            remote(yout_stat.at[at], yin_stat.at[at], hssend.at[at], hsrecv.at[at], peer),
            remote(yout.at[at], yin.at[at], hsend.at[at], hrecv.at[at], peer),
        ))

    def wait_stage(part, k):
        for o in range(8):
            wait_came(("s", part, k, o))

    def ystep(part, step):
        for side in (0, 1):
            k = 0 if step == 0 else 2 * step - 1 + side
            if step > 0 or side == 0:
                wait_stage(part, k)
            for ch in ring_halves(step, side):
                yhop(part, side, step, ch, k)

    def yfinal(part):
        wait_stage(part, 7)
        for ch in (0, 1):
            for side in (0, 1):
                wait_hop(("y", part, side, 3, ch))
            for g in range(3):
                tiles, top, total = merged(part, 7, g, ch)
                parts = [incoming((part, side, 3, ch), g) for side in (0, 1)]
                new_top = jnp.maximum(top, jnp.maximum(parts[0][1], parts[1][1]))
                mine = jnp.exp(top - new_top)
                theirs = [jnp.exp(p[1] - new_top) for p in parts]
                total = total * mine + parts[0][2] * theirs[0] + parts[1][2] * theirs[1]
                share = float(STILES * TILE * NX * NY * NC) / total
                for j in range(half_tiles):
                    value = tiles[j] * mine
                    for side in (0, 1):
                        code = yin[part, side, 3, ch, pl.ds(16 * g, 16), pl.ds(j * TILE, TILE)]
                        value = value + code.astype(F32) * (parts[side][0] * theirs[side])
                    at = (ch * half_tiles + j) * TILE
                    done_ref[pl.ds(48 * part + 16 * g, 16), pl.ds(at, TILE)] = value * share
        early = lax.broadcasted_iota(I32, (8, done_ref.shape[1]), 0) < 4
        for p in (2 * part, 2 * part + 1):
            second = pltpu.roll(done_ref[24 * p + 8 : 24 * p + 16, :], 4, 0)
            mixed = done_ref[24 * p + 16 : 24 * p + 24, :]
            out_ref[24 * p : 24 * p + 8, :] = done_ref[24 * p : 24 * p + 8, :]
            out_ref[24 * p + 8 : 24 * p + 16, :] = jnp.where(early, mixed, second)
            out_ref[24 * p + 16 : 24 * p + 24, :] = jnp.where(early, second, mixed)

    partial(0)
    zstep(0, 0)
    partial(1)
    partial(2)
    zstep(0, 1)
    zstep(1, 0)
    partial(3)
    partial(4)
    zstep(0, 2)
    zstep(1, 1)
    partial(5)
    partial(6)
    zstep(0, 3)
    zstep(1, 2)
    partial(7)
    load_blocks.wait()
    zfinal(0)
    map_and_send(0)
    zstep(1, 3)
    zfinal(1)
    map_and_send(1)
    for o in range(8):
        wait_came(("l", o))
    for part in (0, 1):
        factors(part)
        for step in range(4):
            ystep(part, step)
        yfinal(part)
    for copy in sent:
        copy.wait_send()


def whole(entry, teacher, valid, hidden, head_weight, blocks, labels):
    depth, width = head_weight.shape
    student = STILES * TILE
    dma = pltpu.SemaphoreType.DMA
    smem = pl.BlockSpec(memory_space=pltpu.SMEM)
    vmem = pl.BlockSpec(memory_space=pltpu.VMEM)
    anywhere = pl.BlockSpec(memory_space=pl.ANY)
    ring = (2, 2, 4, 2)
    return pl.pallas_call(
        whole_kernel,
        out_shape=jax.ShapeDtypeStruct((96, student), F32),
        in_specs=[smem, smem, smem, vmem, anywhere, anywhere, anywhere],
        out_specs=vmem,
        scratch_shapes=[
            pltpu.VMEM((depth, width), BF16),
            pltpu.VMEM(blocks.shape, BF16),
            pltpu.VMEM((NX * NY * NC, 16, depth), BF16),
            pltpu.VMEM((8, 96, width), F32),
            pltpu.VMEM(ring + (48, width // 2), I16),
            pltpu.VMEM(ring + (48, width // 2), I16),
            pltpu.VMEM(ring + (16, 128), F32),
            pltpu.VMEM(ring + (16, 128), F32),
            pltpu.VMEM((96, width), F32),
            pltpu.VMEM((2, TEACHER_TILES, 48, TILE), BF16),
            pltpu.VMEM((2, NX * NY * NC * CAP, 48, TILE), BF16),
            pltpu.VMEM((2, 8, 8, CAP, 48, TILE), BF16),
            pltpu.VMEM((8, NY * CAP, 128), F32),
            pltpu.VMEM((2, 16, 128), F32),
            pltpu.VMEM((2, 8, 16, 128), F32),
            pltpu.VMEM((2, 8, 48, TILE), F32),
            pltpu.VMEM((2, 16, 128), F32),
            pltpu.VMEM((96, student), F32),
            pltpu.VMEM(ring + (48, student // 2), I16),
            pltpu.VMEM(ring + (48, student // 2), I16),
            pltpu.VMEM(ring + (16, 128), F32),
            pltpu.VMEM(ring + (16, 128), F32),
            dma, dma, dma, dma((NY,)), dma((NY,)), dma((2, NY)), dma((2, NY)),
            dma((NY,)), dma((NY,)), dma((4, NY)), dma((4, NY)),
            dma(ring), dma(ring), dma(ring), dma(ring),
            dma((2, 8, 8)), dma((2, 8, 8)), dma((8,)), dma((8,)), dma((2, 8)), dma((2, 8)),
            dma(ring), dma(ring), dma(ring), dma(ring),
        ],
        compiler_params=pltpu.CompilerParams(
            collective_id=0, has_side_effects=True, vmem_limit_bytes=VMEM_LIMIT
        ),
        name="whole",
    )(entry, teacher, valid, hidden, head_weight, blocks, labels)


def per_device(hidden_states, head_weight, focus_tiles, focus_blocks):
    hidden = jnp.pad(hidden_states, ((0, 16 - hidden_states.shape[0]), (0, 0)))
    entry, teacher, valid, labels = plan(focus_tiles)
    return whole(entry, teacher, valid, hidden, head_weight, focus_blocks, labels)


def solution(mesh):
    return jax.shard_map(
        per_device,
        mesh=mesh,
        in_specs=(P("vocab", "hid"), P("hid", "vocab"), P("vocab", None), P("vocab", None, None)),
        out_specs=P("hid", "vocab"),
        check_vma=False,
    )
```

```python
import functools

import jax
import jax.numpy as jnp
from jax import lax
from jax.experimental import pallas as pl
from jax.experimental.pallas import tpu as pltpu
from jax.sharding import PartitionSpec as P

TILE = 128
STILES = 12
CAP = 2
TEACHER_TILES = 10
NX, NY, NC, NZ = 4, 8, 2, 8
MESH = pl.DeviceIdType.MESH
VMEM_LIMIT = 60 * 1024 * 1024
ORDER = (4, 3, -3, 2, -2, 1, -1, 0)
F32, BF16, I16, I32 = jnp.float32, jnp.bfloat16, jnp.int16, jnp.int32
TINY = 1e-30
FULL = 32767.0


def index_of(x, y, c):
    return (x * NY + y) * NC + c


def my_place():
    v = lax.axis_index("vocab")
    return v // (NY * NC), (v // NC) % NY, v % NC


def to_vocab(x, y, c):
    return {"vocab": index_of(x, y, c)}


def signal_all(peers):
    barrier = pltpu.get_barrier_semaphore()
    for peer in peers:
        pl.semaphore_signal(barrier, inc=1, device_id=peer, device_id_type=MESH)
    pl.semaphore_wait(barrier, len(peers))


def remote(src, dst, send_sem, recv_sem, peer):
    return pltpu.make_async_remote_copy(
        src_ref=src, dst_ref=dst, send_sem=send_sem, recv_sem=recv_sem,
        device_id=peer, device_id_type=MESH,
    )


def coded(value):
    top = jnp.maximum(jnp.max(jnp.abs(value), axis=1, keepdims=True), TINY)
    codes = jnp.round(value * (FULL / top)).astype(I32).astype(I16)
    return codes, top * (1.0 / FULL)


def lane_is(shape, lane):
    return lax.broadcasted_iota(I32, shape, 1) == lane


def ring_halves(step, side):
    return ((side,), (1 - side, side), (0, 1), (0, 1))[step]


def plan_kernel(tiles_ref, hid_ref, entry_ref, teacher_ref, label_ref, padded_ref, count_ref):
    first = lax.axis_index("vocab") * TEACHER_TILES
    rows, depth = hid_ref.shape
    padded_ref[...] = jnp.concatenate(
        [hid_ref[...].astype(F32), jnp.zeros((16 - rows, depth), F32)], axis=0
    ).astype(BF16)
    label_ref[...] = jnp.full(label_ref.shape, -1.0, F32)
    slot_of_lane = (lax.broadcasted_iota(I32, (1, 128), 1) // 16) % CAP

    def clear(i, carry):
        entry_ref[i] = 0
        teacher_ref[i] = TEACHER_TILES
        return carry

    lax.fori_loop(0, NX * NY * NC * CAP, clear, 0, unroll=8)

    def clear_count(i, carry):
        count_ref[i] = 0
        return carry

    lax.fori_loop(0, NX * NY * NC, clear_count, 0, unroll=8)

    def entry(e, carry):
        student = tiles_ref[1, e]
        owner = student // STILES
        label = student - owner * STILES
        rank = count_ref[owner]
        count_ref[owner] = rank + 1
        group = (owner // (NY * NC)) * NC + owner % NC
        row = (owner // NC) % NY
        slot = (group * NY + row) * CAP + rank
        entry_ref[slot] = e
        teacher_ref[slot] = tiles_ref[0, e] - first
        line = label_ref[group, pl.ds(row, 1), :]
        label_ref[group, pl.ds(row, 1), :] = jnp.where(
            slot_of_lane == rank, label.astype(F32), line
        )
        return carry

    lax.fori_loop(0, tiles_ref.shape[1], entry, 0, unroll=4)


def plan(focus_tiles, hidden):
    slots = NX * NY * NC * CAP
    smem = pl.BlockSpec(memory_space=pltpu.SMEM)
    vmem = pl.BlockSpec(memory_space=pltpu.VMEM)
    return pl.pallas_call(
        plan_kernel,
        out_shape=(
            jax.ShapeDtypeStruct((slots,), I32),
            jax.ShapeDtypeStruct((slots,), I32),
            jax.ShapeDtypeStruct((NX * NC, NY, 128), F32),
            jax.ShapeDtypeStruct((16, hidden.shape[1]), BF16),
        ),
        in_specs=[smem, vmem],
        out_specs=(smem, smem, vmem, vmem),
        scratch_shapes=[pltpu.SMEM((NX * NY * NC,), I32)],
        name="plan",
    )(focus_tiles.T, hidden)


def whole_kernel(
    entry_ref, teacher_ref, hid_ref, w_hbm, blocks_hbm, label_hbm, out_ref,
    w_ref, blocks_ref, all_ref, part_ref, zout, zin, zout_scale, zin_scale, logits_ref,
    weights_ref, slots_ref, slots_in, label_in, top_ref, top_in, total_ref, total_in, group_ref,
    pick_ref, merged_ref, done_ref, yout, yin, yout_stat, yin_stat,
    w_sem, blocks_sem, own_sem, ysend, yrecv, xsend, xrecv, rsend, rrecv, csend, crecv,
    zsend, zrecv, zssend, zsrecv, ssend, srecv, lsend, lrecv, tsend, trecv, usend, urecv,
    hsend, hrecv, hssend, hsrecv,
):
    x, y, c = my_place()
    z = lax.axis_index("hid")
    load_w = pltpu.make_async_copy(w_hbm, w_ref, w_sem)
    load_w.start()
    load_blocks = pltpu.make_async_copy(blocks_hbm, blocks_ref, blocks_sem)
    load_blocks.start()
    xs = ((x + 1) % NX, (x + NX - 1) % NX)
    ys = ((y + 1) % NY, (y + NY - 1) % NY)
    zs = ((z + 1) % NZ, (z + NZ - 1) % NZ)

    def place(o):
        return (x + o // 2) % NX, (c + o % 2) % NC

    def place_vocab(o):
        px, pc = place(o)
        return to_vocab(px, y, pc)

    peers = [to_vocab(x, (y + d) % NY, c) for d in range(1, NY)]
    peers += [place_vocab(o) for o in range(1, 8)]
    peers += [{"hid": n} for n in zs]
    signal_all(peers)

    me = index_of(x, y, c)
    sent = []
    arrived = {}

    def send(src, block, send_sem, recv_sem, peer):
        copy = remote(src, all_ref.at[block], send_sem, recv_sem, peer)
        copy.start()
        sent.append(copy)
        return copy

    for d in (4, 3, 5, 2, 6, 1, 7):
        arrived["y", d] = send(
            hid_ref, me, ysend.at[d], yrecv.at[d], to_vocab(x, (y + d) % NY, c)
        )
    own = pltpu.make_async_copy(hid_ref, all_ref.at[me], own_sem)
    own.start()
    for d in (0, 1, 7, 2, 6, 3, 5, 4):
        block = index_of(x, (y + NY - d) % NY, c)
        src = all_ref.at[block]
        if d == 0:
            src = hid_ref
        else:
            arrived["y", d].wait_recv()
        for side in (0, 1):
            arrived["x", side, d] = send(
                src, block, xsend.at[side, d], xrecv.at[side, d], to_vocab(xs[side], y, c)
            )
        arrived["c", 0, d] = send(
            src, block, csend.at[0, d], crecv.at[0, d], to_vocab(x, y, 1 - c)
        )
    for d in (0, 1, 7, 2, 6, 3, 5, 4):
        for side in (0, 1):
            arrived["x", side, d].wait_recv()
            block = index_of(xs[1 - side], (y + NY - d) % NY, c)
            src = all_ref.at[block]
            if d % 2 == side:
                arrived["r", d] = send(
                    src, block, rsend.at[d], rrecv.at[d], to_vocab(xs[side], y, c)
                )
            arrived["c", 1 + side, d] = send(
                src, block, csend.at[1 + side, d], crecv.at[1 + side, d],
                to_vocab(x, y, 1 - c),
            )
    for d in (0, 1, 7, 2, 6, 3, 5, 4):
        arrived["r", d].wait_recv()
        block = index_of((x + 2) % NX, (y + NY - d) % NY, c)
        arrived["c", 3, d] = send(
            all_ref.at[block], block, csend.at[3, d], crecv.at[3, d],
            to_vocab(x, y, 1 - c),
        )
    own.wait()
    load_w.wait()
    for kind in range(4):
        for d in range(NY):
            arrived["c", kind, d].wait_recv()

    came = {}
    for o in range(8):
        px, pc = place(o)
        src = label_hbm.at[px * NC + pc]
        if o == 0:
            copy = pltpu.make_async_copy(src, label_in.at[0], lrecv.at[0])
        else:
            copy = remote(src, label_in.at[o], lsend.at[o], lrecv.at[o], place_vocab(o))
            sent.append(copy)
        copy.start()
        came["l", o] = copy

    def wait_came(key):
        if key[-1] == 0:
            came[key].wait()
        else:
            came[key].wait_recv()

    columns = 256

    def partial(k):
        target = (z + ORDER[k] + NZ) % NZ
        rows = all_ref[pl.ds(target * 8, 8)].reshape(128, all_ref.shape[2])

        def body(n, carry):
            at = pl.ds(pl.multiple_of(n * columns, columns), columns)
            p = jnp.dot(rows, w_ref[:, at], preferred_element_type=F32)
            for i in range(4):
                q = p[32 * i : 32 * i + 32]
                part_ref[k, pl.ds(24 * i, 8), at] = q[0:8]
                part_ref[k, pl.ds(24 * i + 8, 8), at] = q[16:24]
                part_ref[k, pl.ds(24 * i + 16, 8), at] = q[8:16] + pltpu.roll(q[24:32], 4, 0)
            return carry

        lax.fori_loop(0, w_ref.shape[1] // columns, body, 0)

    zhalf = w_ref.shape[1] // 2
    hops = {}

    def send_hop(key, copies):
        for copy in copies:
            copy.start()
            sent.append(copy)
        hops[key] = copies

    def wait_hop(key):
        for copy in hops[key]:
            copy.wait_recv()

    def zvalue(at, g):
        return zin[at + (pl.ds(16 * g, 16),)].astype(F32) * zin_scale[at][:, g : g + 1]

    def zhop(part, side, step, ch, k):
        at = (part, side, step, ch)
        before = (part, side, step - 1, ch)
        has_input = step >= 1 and ch in ring_halves(step - 1, side)
        if has_input:
            wait_hop(("z",) + before)
        scales = jnp.zeros((16, 128), F32)
        for g in range(3):
            value = part_ref[k, pl.ds(48 * part + 16 * g, 16), ch * zhalf : (ch + 1) * zhalf]
            if has_input:
                value = value + zvalue(before, g)
            codes, scale = coded(value)
            zout[at + (pl.ds(16 * g, 16),)] = codes
            scales = jnp.where(lane_is((16, 128), g), scale, scales)
        zout_scale[at] = scales
        peer = {"hid": zs[side]}
        send_hop(("z",) + at, (
            remote(zout_scale.at[at], zin_scale.at[at], zssend.at[at], zsrecv.at[at], peer),
            remote(zout.at[at], zin.at[at], zsend.at[at], zrecv.at[at], peer),
        ))

    def zstep(part, step):
        for turn in (0, 1):
            for side in (0, 1):
                if turn < len(ring_halves(step, side)):
                    k = 0 if step == 0 else 2 * step - 1 + side
                    zhop(part, side, step, ring_halves(step, side)[turn], k)

    def zfinal(part):
        for ch in (0, 1):
            cols = slice(ch * zhalf, (ch + 1) * zhalf)
            for side in (0, 1):
                wait_hop(("z", part, side, 3, ch))
            for g in range(3):
                rows = pl.ds(48 * part + 16 * g, 16)
                logits_ref[rows, cols] = (
                    part_ref[7, rows, cols]
                    + zvalue((part, 0, 3, ch), g)
                    + zvalue((part, 1, 3, ch), g)
                )

    def to_group(name, part, src, into, send_sem, recv_sem):
        for o in range(8):
            dst = into.at[part, o]
            if o == 0:
                copy = pltpu.make_async_copy(src, dst, recv_sem.at[part, 0])
            else:
                copy = remote(
                    src, dst, send_sem.at[part, o], recv_sem.at[part, o], place_vocab(o)
                )
                sent.append(copy)
            copy.start()
            came[name, part, o] = copy

    def send_tops(part):
        tops = jnp.zeros((16, 128), F32)
        for g in range(3):
            top = jnp.max(logits_ref[pl.ds(48 * part + 16 * g, 16), :], axis=1, keepdims=True)
            tops = jnp.where(lane_is((16, 128), g), top, tops)
        top_ref[part] = tops
        to_group("top", part, top_ref.at[part], top_in, tsend, trecv)

    def map_and_send(part):
        for o in range(8):
            wait_came(("top", part, o))
        tops = functools.reduce(jnp.maximum, [top_in[part, o] for o in range(8)])
        totals = jnp.zeros((16, 128), F32)
        weights_ref[part, TEACHER_TILES] = jnp.zeros((48, TILE), BF16)
        for g in range(3):
            logits = logits_ref[pl.ds(48 * part + 16 * g, 16), :]
            values = jnp.exp(logits - tops[:, g : g + 1])
            total = jnp.sum(values, axis=1, keepdims=True)
            for t in range(TEACHER_TILES):
                weights_ref[part, t, pl.ds(16 * g, 16), :] = values[
                    :, t * TILE : (t + 1) * TILE
                ].astype(BF16)
            totals = jnp.where(lane_is((16, 128), 8 + g), total, totals)
        total_ref[part] = totals
        to_group("total", part, total_ref.at[part], total_in, usend, urecv)
        for k in range(8):
            row = (y + ORDER[k] + NY) % NY

            def products(o, carry, row=row):
                base = (((x + o // 2) % NX * NC + (c + o % 2) % NC) * NY + row) * CAP
                for i in range(CAP):
                    product = jnp.dot(
                        weights_ref[part, teacher_ref[base + i]],
                        blocks_ref[entry_ref[base + i]],
                        preferred_element_type=F32,
                    )
                    slots_ref[part, base + i] = product.astype(BF16)
                return carry

            lax.fori_loop(0, 8, products, 0, unroll=4)
            for o in (4, 5, 2, 6, 3, 7, 1, 0):
                px, pc = place(o)
                src = slots_ref.at[part, pl.ds(((px * NC + pc) * NY + row) * CAP, CAP)]
                at = (part, k, o)
                if o == 0:
                    copy = pltpu.make_async_copy(src, slots_in.at[at], srecv.at[at])
                else:
                    copy = remote(
                        src, slots_in.at[at], ssend.at[at], srecv.at[at], place_vocab(o)
                    )
                    sent.append(copy)
                copy.start()
                came[("s",) + at] = copy

    def group_stats(part):
        for o in range(8):
            wait_came(("total", part, o))
        tops = functools.reduce(jnp.maximum, [top_in[part, o] for o in range(8)])
        totals = functools.reduce(jnp.add, [total_in[part, o] for o in range(8)])
        lanes = lax.broadcasted_iota(I32, (16, 128), 1)
        group_ref[part] = jnp.where(lanes < 8, tops, totals)

    def pick(k):
        row = (y + ORDER[k] + NY) % NY
        shape = (STILES * 16, 128)
        lines = lax.broadcasted_iota(I32, shape, 0)
        lanes = lax.broadcasted_iota(I32, shape, 1)
        tile = (lines // 16).astype(F32)
        same_position = lines % 16 == lanes % 16
        quarter = lax.broadcasted_iota(I32, (1, 128), 1) // 32
        for side in (0, 1):
            labels = label_in[4 * side, pl.ds(row, 1), :]
            for q in range(1, 4):
                labels = jnp.where(quarter == q, label_in[4 * side + q, pl.ds(row, 1), :], labels)
            chosen = jnp.logical_and(same_position, tile == labels)
            pick_ref[k, :, 128 * side : 128 * (side + 1)] = jnp.where(
                chosen, 1.0, 0.0
            ).astype(BF16)

    def merge(part, k):
        for o in range(8):
            wait_came(("s", part, k, o))
        for g in range(3):
            slots = slots_in[part, k, :, :, pl.ds(16 * g, 16), :].reshape(16 * 16, TILE)
            tiles = jnp.dot(pick_ref[k], slots, preferred_element_type=F32)
            for j in range(STILES):
                merged_ref[part, k, pl.ds(16 * g, 16), pl.ds(j * TILE, TILE)] = tiles[
                    16 * j : 16 * (j + 1)
                ]

    yhalf = STILES * TILE // 2

    def merged(part, k, g, ch):
        group = group_ref[part]
        tiles = merged_ref[part, k, pl.ds(16 * g, 16), pl.ds(ch * yhalf, yhalf)]
        return tiles, group[:, g : g + 1], group[:, 8 + g : 9 + g]

    def incoming(at, g):
        stat = yin_stat[at]
        return stat[:, g : g + 1], stat[:, 8 + g : 9 + g], stat[:, 16 + g : 17 + g]

    def yhop(part, side, step, ch, k):
        at = (part, side, step, ch)
        before = (part, side, step - 1, ch)
        has_input = step >= 1 and ch in ring_halves(step - 1, side)
        if has_input:
            wait_hop(("y",) + before)
        stats = jnp.zeros((16, 128), F32)
        for g in range(3):
            tiles, top, total = merged(part, k, g, ch)
            if has_input:
                scale, in_top, in_total = incoming(before, g)
                new_top = jnp.maximum(top, in_top)
                mine = jnp.exp(top - new_top)
                theirs = jnp.exp(in_top - new_top)
                total = total * mine + in_total * theirs
                scale = scale * theirs
                top = new_top
                code = yin[before + (pl.ds(16 * g, 16),)]
                tiles = tiles * mine + code.astype(F32) * scale
            codes, scale = coded(tiles)
            yout[at + (pl.ds(16 * g, 16),)] = codes
            stats = jnp.where(lane_is((16, 128), g), scale, stats)
            stats = jnp.where(lane_is((16, 128), 8 + g), top, stats)
            stats = jnp.where(lane_is((16, 128), 16 + g), total, stats)
        yout_stat[at] = stats
        peer = to_vocab(x, ys[side], c)
        send_hop(("y",) + at, (
            remote(yout_stat.at[at], yin_stat.at[at], hssend.at[at], hsrecv.at[at], peer),
            remote(yout.at[at], yin.at[at], hsend.at[at], hrecv.at[at], peer),
        ))

    def ystep(part, step):
        for side in (0, 1):
            k = 0 if step == 0 else 2 * step - 1 + side
            if step > 0 or side == 0:
                merge(part, k)
            for ch in ring_halves(step, side):
                yhop(part, side, step, ch, k)

    def yfinal(part):
        merge(part, 7)
        for ch in (0, 1):
            for side in (0, 1):
                wait_hop(("y", part, side, 3, ch))
            for g in range(3):
                tiles, top, total = merged(part, 7, g, ch)
                parts = [incoming((part, side, 3, ch), g) for side in (0, 1)]
                new_top = jnp.maximum(top, jnp.maximum(parts[0][1], parts[1][1]))
                mine = jnp.exp(top - new_top)
                theirs = [jnp.exp(p[1] - new_top) for p in parts]
                total = total * mine + parts[0][2] * theirs[0] + parts[1][2] * theirs[1]
                share = float(STILES * TILE * NX * NY * NC) / total
                value = tiles * mine
                for side in (0, 1):
                    code = yin[part, side, 3, ch, pl.ds(16 * g, 16), :]
                    value = value + code.astype(F32) * (parts[side][0] * theirs[side])
                done_ref[pl.ds(48 * part + 16 * g, 16), pl.ds(ch * yhalf, yhalf)] = value * share
        early = lax.broadcasted_iota(I32, (8, done_ref.shape[1]), 0) < 4
        for p in (2 * part, 2 * part + 1):
            second = pltpu.roll(done_ref[24 * p + 8 : 24 * p + 16, :], 4, 0)
            mixed = done_ref[24 * p + 16 : 24 * p + 24, :]
            out_ref[24 * p : 24 * p + 8, :] = done_ref[24 * p : 24 * p + 8, :]
            out_ref[24 * p + 8 : 24 * p + 16, :] = jnp.where(early, mixed, second)
            out_ref[24 * p + 16 : 24 * p + 24, :] = jnp.where(early, second, mixed)

    partial(0)
    zstep(0, 0)
    partial(1)
    partial(2)
    zstep(0, 1)
    zstep(1, 0)
    partial(3)
    partial(4)
    zstep(0, 2)
    zstep(1, 1)
    partial(5)
    partial(6)
    zstep(0, 3)
    partial(7)
    load_blocks.wait()
    zfinal(0)
    send_tops(0)
    zstep(1, 2)
    map_and_send(0)
    zstep(1, 3)
    for o in range(8):
        wait_came(("l", o))
    for k in range(8):
        pick(k)
    zfinal(1)
    send_tops(1)
    group_stats(0)
    ystep(0, 0)
    map_and_send(1)
    for step in range(1, 4):
        ystep(0, step)
    group_stats(1)
    ystep(1, 0)
    yfinal(0)
    for step in range(1, 4):
        ystep(1, step)
    yfinal(1)
    for copy in sent:
        copy.wait_send()


def whole(entry, teacher, hidden, head_weight, blocks, labels):
    depth, width = head_weight.shape
    student = STILES * TILE
    dma = pltpu.SemaphoreType.DMA
    smem = pl.BlockSpec(memory_space=pltpu.SMEM)
    vmem = pl.BlockSpec(memory_space=pltpu.VMEM)
    anywhere = pl.BlockSpec(memory_space=pl.ANY)
    ring = (2, 2, 4, 2)
    return pl.pallas_call(
        whole_kernel,
        out_shape=jax.ShapeDtypeStruct((96, student), F32),
        in_specs=[smem, smem, vmem, anywhere, anywhere, anywhere],
        out_specs=vmem,
        scratch_shapes=[
            pltpu.VMEM((depth, width), BF16),
            pltpu.VMEM(blocks.shape, BF16),
            pltpu.VMEM((NX * NY * NC, 16, depth), BF16),
            pltpu.VMEM((8, 96, width), F32),
            pltpu.VMEM(ring + (48, width // 2), I16),
            pltpu.VMEM(ring + (48, width // 2), I16),
            pltpu.VMEM(ring + (16, 128), F32),
            pltpu.VMEM(ring + (16, 128), F32),
            pltpu.VMEM((96, width), F32),
            pltpu.VMEM((2, TEACHER_TILES + 1, 48, TILE), BF16),
            pltpu.VMEM((2, NX * NY * NC * CAP, 48, TILE), BF16),
            pltpu.VMEM((2, 8, 8, CAP, 48, TILE), BF16),
            pltpu.VMEM((8, NY, 128), F32),
            pltpu.VMEM((2, 16, 128), F32),
            pltpu.VMEM((2, 8, 16, 128), F32),
            pltpu.VMEM((2, 16, 128), F32),
            pltpu.VMEM((2, 8, 16, 128), F32),
            pltpu.VMEM((2, 16, 128), F32),
            pltpu.VMEM((8, STILES * 16, 256), BF16),
            pltpu.VMEM((2, 8, 48, student), F32),
            pltpu.VMEM((96, student), F32),
            pltpu.VMEM(ring + (48, student // 2), I16),
            pltpu.VMEM(ring + (48, student // 2), I16),
            pltpu.VMEM(ring + (16, 128), F32),
            pltpu.VMEM(ring + (16, 128), F32),
            dma, dma, dma, dma((NY,)), dma((NY,)), dma((2, NY)), dma((2, NY)),
            dma((NY,)), dma((NY,)), dma((4, NY)), dma((4, NY)),
            dma(ring), dma(ring), dma(ring), dma(ring),
            dma((2, 8, 8)), dma((2, 8, 8)), dma((8,)), dma((8,)), dma((2, 8)), dma((2, 8)),
            dma((2, 8)), dma((2, 8)),
            dma(ring), dma(ring), dma(ring), dma(ring),
        ],
        compiler_params=pltpu.CompilerParams(
            collective_id=0, has_side_effects=True, vmem_limit_bytes=VMEM_LIMIT
        ),
        name="whole",
    )(entry, teacher, hidden, head_weight, blocks, labels)


def per_device(hidden_states, head_weight, focus_tiles, focus_blocks):
    entry, teacher, labels, hidden = plan(focus_tiles, hidden_states)
    return whole(entry, teacher, hidden, head_weight, focus_blocks, labels)


def solution(mesh):
    return jax.shard_map(
        per_device,
        mesh=mesh,
        in_specs=(P("vocab", "hid"), P("hid", "vocab"), P("vocab", None), P("vocab", None, None)),
        out_specs=P("hid", "vocab"),
        check_vma=False,
    )
```

```python
import functools

import jax
import jax.numpy as jnp
from jax import lax
from jax.experimental import pallas as pl
from jax.experimental.pallas import tpu as pltpu
from jax.sharding import PartitionSpec as P

TILE = 128
STILES = 12
CAP = 2
NX, NY, NC, NZ = 4, 8, 2, 8
MESH = pl.DeviceIdType.MESH
VMEM_LIMIT = 60 * 1024 * 1024
ORDER = (4, 3, -3, 2, -2, 1, -1, 0)
F32, BF16, I16, I32 = jnp.float32, jnp.bfloat16, jnp.int16, jnp.int32
TINY = 1e-30
FULL = 32767.0


def index_of(x, y, c):
    return (x * NY + y) * NC + c


def my_place():
    v = lax.axis_index("vocab")
    return v // (NY * NC), (v // NC) % NY, v % NC


def to_vocab(x, y, c):
    return {"vocab": index_of(x, y, c)}


def signal_all(peers):
    barrier = pltpu.get_barrier_semaphore()
    for peer in peers:
        pl.semaphore_signal(barrier, inc=1, device_id=peer, device_id_type=MESH)
    pl.semaphore_wait(barrier, len(peers))


def remote(src, dst, send_sem, recv_sem, peer):
    return pltpu.make_async_remote_copy(
        src_ref=src, dst_ref=dst, send_sem=send_sem, recv_sem=recv_sem,
        device_id=peer, device_id_type=MESH,
    )


def coded(value):
    top = jnp.maximum(jnp.max(jnp.abs(value), axis=1, keepdims=True), TINY)
    codes = jnp.round(value * (FULL / top)).astype(I32).astype(I16)
    return codes, top * (1.0 / FULL)


def lane_is(shape, lane):
    return lax.broadcasted_iota(I32, shape, 1) == lane


def ring_halves(step, side):
    if step == 0:
        return (0,) if side == 0 else (1,)
    return (0, 1)


def gather_logits_kernel(
    rows_ref, w_hbm, out_ref, hid_ref, w_ref, all_ref, part_ref,
    out_code, in_code, out_scale, in_scale,
    w_sem, own_sem, ysend, yrecv, xsend, xrecv, rsend, rrecv, csend, crecv,
    zsend, zrecv, zssend, zsrecv,
):
    x, y, c = my_place()
    z = lax.axis_index("hid")
    load_w = pltpu.make_async_copy(w_hbm, w_ref, w_sem)
    load_w.start()
    count, depth = rows_ref.shape
    hid_ref[...] = jnp.concatenate(
        [rows_ref[...].astype(F32), jnp.zeros((16 - count, depth), F32)], axis=0
    ).astype(BF16)
    xs = ((x + 1) % NX, (x + NX - 1) % NX)
    zs = ((z + 1) % NZ, (z + NZ - 1) % NZ)
    peers = [to_vocab(x, (y + d) % NY, c) for d in range(1, NY)]
    peers += [to_vocab(n, y, c) for n in xs] + [to_vocab(x, y, 1 - c)]
    peers += [{"hid": n} for n in zs]
    signal_all(peers)

    me = index_of(x, y, c)
    sent = []
    arrived = {}

    def send(src, block, send_sem, recv_sem, peer):
        copy = remote(src, all_ref.at[block], send_sem, recv_sem, peer)
        copy.start()
        sent.append(copy)
        return copy

    for d in (4, 3, 5, 2, 6, 1, 7):
        arrived["y", d] = send(
            hid_ref, me, ysend.at[d], yrecv.at[d], to_vocab(x, (y + d) % NY, c)
        )
    own = pltpu.make_async_copy(hid_ref, all_ref.at[me], own_sem)
    own.start()
    for d in (0, 1, 7, 2, 6, 3, 5, 4):
        block = index_of(x, (y + NY - d) % NY, c)
        src = all_ref.at[block]
        if d == 0:
            src = hid_ref
        else:
            arrived["y", d].wait_recv()
        for side in (0, 1):
            arrived["x", side, d] = send(
                src, block, xsend.at[side, d], xrecv.at[side, d], to_vocab(xs[side], y, c)
            )
        arrived["c", 0, d] = send(
            src, block, csend.at[0, d], crecv.at[0, d], to_vocab(x, y, 1 - c)
        )
    for d in (0, 1, 7, 2, 6, 3, 5, 4):
        for side in (0, 1):
            arrived["x", side, d].wait_recv()
            block = index_of(xs[1 - side], (y + NY - d) % NY, c)
            src = all_ref.at[block]
            if d % 2 == side:
                arrived["r", d] = send(
                    src, block, rsend.at[d], rrecv.at[d], to_vocab(xs[side], y, c)
                )
            arrived["c", 1 + side, d] = send(
                src, block, csend.at[1 + side, d], crecv.at[1 + side, d],
                to_vocab(x, y, 1 - c),
            )
    for d in (0, 1, 7, 2, 6, 3, 5, 4):
        arrived["r", d].wait_recv()
        block = index_of((x + 2) % NX, (y + NY - d) % NY, c)
        arrived["c", 3, d] = send(
            all_ref.at[block], block, csend.at[3, d], crecv.at[3, d],
            to_vocab(x, y, 1 - c),
        )
    own.wait()
    load_w.wait()
    for kind in range(4):
        for d in range(NY):
            arrived["c", kind, d].wait_recv()

    columns = 256

    def partial(k):
        target = (z + ORDER[k] + NZ) % NZ
        rows = all_ref[pl.ds(target * 8, 8)].reshape(128, all_ref.shape[2])

        def body(n, carry):
            at = pl.ds(pl.multiple_of(n * columns, columns), columns)
            p = jnp.dot(rows, w_ref[:, at], preferred_element_type=F32)
            for i in range(4):
                q = p[32 * i : 32 * i + 32]
                part_ref[k, pl.ds(24 * i, 8), at] = q[0:8]
                part_ref[k, pl.ds(24 * i + 8, 8), at] = q[16:24]
                part_ref[k, pl.ds(24 * i + 16, 8), at] = q[8:16] + pltpu.roll(q[24:32], 4, 0)
            return carry

        lax.fori_loop(0, w_ref.shape[1] // columns, body, 0)

    def decoded(side, step, half, g):
        scale = in_scale[side, step, half][:, g : g + 1]
        return in_code[side, step, half, pl.ds(16 * g, 16), :].astype(F32) * scale

    hops = {}

    def wait_hop(side, step, half):
        for copy in hops[side, step, half]:
            copy.wait_recv()

    def hop(side, step, half, k):
        has_input = step >= 1 and half in ring_halves(step - 1, side)
        if has_input:
            wait_hop(side, step - 1, half)
        scales = jnp.zeros((16, 128), F32)
        for g in range(3):
            value = part_ref[k, pl.ds(48 * half + 16 * g, 16), :]
            if has_input:
                value = value + decoded(side, step - 1, half, g)
            codes, scale = coded(value)
            out_code[side, step, half, pl.ds(16 * g, 16), :] = codes
            scales = jnp.where(lane_is((16, 128), g), scale, scales)
        out_scale[side, step, half] = scales
        peer = {"hid": zs[side]}
        copies = (
            remote(out_scale.at[side, step, half], in_scale.at[side, step, half],
                   zssend.at[side, step, half], zsrecv.at[side, step, half], peer),
            remote(out_code.at[side, step, half], in_code.at[side, step, half],
                   zsend.at[side, step, half], zrecv.at[side, step, half], peer),
        )
        for copy in copies:
            copy.start()
            sent.append(copy)
        hops[side, step, half] = copies

    partial(0)
    for step in range(4):
        for half in (0, 1):
            for side in (0, 1):
                now = half if step != 1 else (half + 1 - side) % 2
                if now in ring_halves(step, side):
                    hop(side, step, now, 0 if step == 0 else 2 * step - 1 + side)
        if step < 3:
            partial(2 * step + 1)
            partial(2 * step + 2)
    partial(7)
    for half in (0, 1):
        for side in (0, 1):
            wait_hop(side, 3, half)
        for g in range(3):
            at = pl.ds(48 * half + 16 * g, 16)
            out_ref[at, :] = (
                part_ref[7, at, :] + decoded(0, 3, half, g) + decoded(1, 3, half, g)
            )
    for copy in sent:
        copy.wait_send()


def gather_logits(hidden, head_weight):
    depth, width = head_weight.shape
    dma = pltpu.SemaphoreType.DMA
    return pl.pallas_call(
        gather_logits_kernel,
        out_shape=jax.ShapeDtypeStruct((96, width), F32),
        in_specs=[
            pl.BlockSpec(memory_space=pltpu.VMEM),
            pl.BlockSpec(memory_space=pl.ANY),
        ],
        out_specs=pl.BlockSpec(memory_space=pltpu.VMEM),
        scratch_shapes=[
            pltpu.VMEM((16, depth), BF16),
            pltpu.VMEM((depth, width), BF16),
            pltpu.VMEM((NX * NY * NC, 16, depth), BF16),
            pltpu.VMEM((8, 96, width), F32),
            pltpu.VMEM((2, 4, 2, 48, width), I16),
            pltpu.VMEM((2, 4, 2, 48, width), I16),
            pltpu.VMEM((2, 4, 2, 16, 128), F32),
            pltpu.VMEM((2, 4, 2, 16, 128), F32),
            dma, dma, dma((NY,)), dma((NY,)), dma((2, NY)), dma((2, NY)),
            dma((NY,)), dma((NY,)), dma((4, NY)), dma((4, NY)),
            dma((2, 4, 2)), dma((2, 4, 2)), dma((2, 4, 2)), dma((2, 4, 2)),
        ],
        compiler_params=pltpu.CompilerParams(
            collective_id=0, has_side_effects=True, vmem_limit_bytes=VMEM_LIMIT
        ),
        name="gather_logits",
    )(hidden, head_weight)


def map_tiles_kernel(tiles_ref, logits_ref, blocks_ref, slots_ref, meta_ref, weights_ref, count_ref):
    teacher_tiles = logits_ref.shape[1] // TILE
    first = lax.axis_index("vocab") * teacher_tiles
    stats = jnp.zeros((6, 16, 128), F32)
    pieces = []
    for g in range(6):
        rows = pl.ds(16 * g, 16)
        logits = logits_ref[rows, :]
        top = jnp.max(logits, axis=1, keepdims=True)
        values = jnp.exp(logits - top)
        total = jnp.sum(values, axis=1, keepdims=True)
        for t in range(teacher_tiles):
            weights_ref[t, rows, :] = values[:, t * TILE : (t + 1) * TILE].astype(BF16)
        pieces.append((top, total))
    stats = jnp.zeros((16, 128), F32)
    for g, (top, total) in enumerate(pieces):
        stats = jnp.where(lane_is((16, 128), g), top, stats)
        stats = jnp.where(lane_is((16, 128), 8 + g), total, stats)
    for d in range(8):
        meta_ref[d, 0:16, :] = jnp.full((16, 128), -1.0, F32)
        meta_ref[d, 16:32, :] = stats

    def clear(i, carry):
        slots_ref[i] = jnp.zeros((96, TILE), BF16)
        return carry

    lax.fori_loop(0, slots_ref.shape[0], clear, 0, unroll=8)

    def clear_count(i, carry):
        count_ref[i] = 0
        return carry

    lax.fori_loop(0, count_ref.shape[0], clear_count, 0, unroll=8)

    def entry(e, carry):
        student = tiles_ref[1, e]
        owner = student // STILES
        label = student - owner * STILES
        rank = count_ref[owner]
        count_ref[owner] = rank + 1
        group = (owner // (NY * NC)) * NC + owner % NC
        line = ((owner // NC) % NY) * CAP + rank
        product = jnp.dot(
            weights_ref[tiles_ref[0, e] - first], blocks_ref[e], preferred_element_type=F32
        )
        slots_ref[group * (NY * CAP) + line] = product.astype(BF16)
        meta_ref[group, pl.ds(line, 1), :] = jnp.full((1, 128), label.astype(F32))
        return carry

    lax.fori_loop(0, tiles_ref.shape[1], entry, 0, unroll=8)


def map_tiles(focus_tiles, logits, focus_blocks):
    groups = NX * NC
    return pl.pallas_call(
        map_tiles_kernel,
        out_shape=(
            jax.ShapeDtypeStruct((groups * NY * CAP, 96, TILE), BF16),
            jax.ShapeDtypeStruct((groups, 32, 128), F32),
        ),
        in_specs=[
            pl.BlockSpec(memory_space=pltpu.SMEM),
            pl.BlockSpec(memory_space=pltpu.VMEM),
            pl.BlockSpec(memory_space=pltpu.VMEM),
        ],
        out_specs=(
            pl.BlockSpec(memory_space=pltpu.VMEM),
            pl.BlockSpec(memory_space=pltpu.VMEM),
        ),
        scratch_shapes=[
            pltpu.VMEM((logits.shape[1] // TILE, 96, TILE), BF16),
            pltpu.SMEM((NX * NY * NC,), I32),
        ],
        compiler_params=pltpu.CompilerParams(vmem_limit_bytes=VMEM_LIMIT),
        name="map_tiles",
    )(focus_tiles.T, logits, focus_blocks)


def exchange_kernel(
    slots_hbm, meta_hbm, out_ref, slots_in, meta_in, factor_ref, group_ref, done_ref,
    out_code, in_code, out_stat, in_stat,
    ssend, srecv, msend, mrecv, ysend, yrecv, tsend, trecv,
):
    x, y, c = my_place()
    width = STILES * TILE
    ys = ((y + 1) % NY, (y + NY - 1) % NY)

    def place(o):
        return (x + o // 2) % NX, (c + o % 2) % NC

    peers = []
    for o in range(1, 8):
        px, pc = place(o)
        peers.append(to_vocab(px, y, pc))
    peers += [to_vocab(x, n, c) for n in ys]
    signal_all(peers)

    sent = []
    came = {}
    for o in range(8):
        px, pc = place(o)
        src = meta_hbm.at[px * NC + pc]
        if o == 0:
            copy = pltpu.make_async_copy(src, meta_in.at[0], mrecv.at[0])
        else:
            copy = remote(src, meta_in.at[o], msend.at[o], mrecv.at[o], to_vocab(px, y, pc))
            sent.append(copy)
        copy.start()
        came["m", o] = copy
    for k in range(8):
        row = (y + ORDER[k] + NY) % NY
        for o in (4, 5, 2, 6, 3, 7, 1, 0):
            px, pc = place(o)
            src = slots_hbm.at[pl.ds(((px * NC + pc) * NY + row) * CAP, CAP)]
            if o == 0:
                copy = pltpu.make_async_copy(src, slots_in.at[k, 0], srecv.at[k, 0])
            else:
                copy = remote(
                    src, slots_in.at[k, o], ssend.at[k, o], srecv.at[k, o],
                    to_vocab(px, y, pc),
                )
                sent.append(copy)
            copy.start()
            came[k, o] = copy

    def wait_came(key):
        if key[1] == 0:
            came[key].wait()
        else:
            came[key].wait_recv()

    for o in range(8):
        wait_came(("m", o))
    groups = jnp.zeros((16, 128), F32)
    for g in range(6):
        tops = [meta_in[o, 16:32, g : g + 1] for o in range(8)]
        top = functools.reduce(jnp.maximum, tops)
        total = jnp.zeros((16, 1), F32)
        for o in range(8):
            factor = jnp.exp(tops[o] - top)
            total = total + factor * meta_in[o, 16:32, 8 + g : 9 + g]
            factor_ref[o, pl.ds(16 * g, 16), :] = jnp.broadcast_to(factor, (16, 128))
        groups = jnp.where(lane_is((16, 128), g), top, groups)
        groups = jnp.where(lane_is((16, 128), 8 + g), total, groups)
    group_ref[...] = groups

    def merged(k, at):
        row = (y + ORDER[k] + NY) % NY
        tiles = [jnp.zeros((16, TILE), F32)] * STILES
        for o in range(8):
            factor = factor_ref[o, at, :]
            for i in range(CAP):
                tile = slots_in[k, o, i, at, :].astype(F32) * factor
                label = meta_in[o, pl.ds(row * CAP + i, 1), :]
                for j in range(STILES):
                    tiles[j] = tiles[j] + jnp.where(label == float(j), tile, 0.0)
        return tiles

    hops = {}

    def wait_hop(side, step, half):
        for copy in hops[side, step, half]:
            copy.wait_recv()

    def incoming(side, step, half, g):
        stat = in_stat[side, step, half]
        return stat[:, g : g + 1], stat[:, 8 + g : 9 + g], stat[:, 16 + g : 17 + g]

    def hop(side, step, half, k):
        has_input = step >= 1 and half in ring_halves(step - 1, side)
        if has_input:
            wait_hop(side, step - 1, half)
        stats = jnp.zeros((16, 128), F32)
        for g in range(3):
            row_at = pl.ds(48 * half + 16 * g, 16)
            code_at = pl.ds(16 * g, 16)
            tiles = merged(k, row_at)
            lane = 3 * half + g
            top = group_ref[:, lane : lane + 1]
            total = group_ref[:, 8 + lane : 9 + lane]
            if has_input:
                scale, in_top, in_total = incoming(side, step - 1, half, g)
                new_top = jnp.maximum(top, in_top)
                mine = jnp.exp(top - new_top)
                theirs = jnp.exp(in_top - new_top)
                total = total * mine + in_total * theirs
                scale = scale * theirs
                top = new_top
                for j in range(STILES):
                    code = in_code[side, step - 1, half, code_at, j * TILE : (j + 1) * TILE]
                    tiles[j] = tiles[j] * mine + code.astype(F32) * scale
            codes, scale = coded(jnp.concatenate(tiles, axis=1))
            out_code[side, step, half, code_at, :] = codes
            stats = jnp.where(lane_is((16, 128), g), scale, stats)
            stats = jnp.where(lane_is((16, 128), 8 + g), top, stats)
            stats = jnp.where(lane_is((16, 128), 16 + g), total, stats)
        out_stat[side, step, half] = stats
        peer = to_vocab(x, ys[side], c)
        copies = (
            remote(out_stat.at[side, step, half], in_stat.at[side, step, half],
                   tsend.at[side, step, half], trecv.at[side, step, half], peer),
            remote(out_code.at[side, step, half], in_code.at[side, step, half],
                   ysend.at[side, step, half], yrecv.at[side, step, half], peer),
        )
        for copy in copies:
            copy.start()
            sent.append(copy)
        hops[side, step, half] = copies

    def wait_stage(k):
        for o in range(8):
            wait_came((k, o))

    for step in range(4):
        if step == 0:
            wait_stage(0)
            hop(0, 0, 0, 0)
            hop(1, 0, 1, 0)
        else:
            for side in (0, 1):
                k = 2 * step - 1 + side
                wait_stage(k)
                fresh = 1 if side == 0 else 0
                order = (fresh, 1 - fresh) if step == 1 else (0, 1)
                for half in order:
                    hop(side, step, half, k)
    wait_stage(7)
    for half in (0, 1):
        for side in (0, 1):
            wait_hop(side, 3, half)
        for g in range(3):
            row_at = pl.ds(48 * half + 16 * g, 16)
            code_at = pl.ds(16 * g, 16)
            tiles = merged(7, row_at)
            lane = 3 * half + g
            top = group_ref[:, lane : lane + 1]
            total = group_ref[:, 8 + lane : 9 + lane]
            parts = [incoming(side, 3, half, g) for side in (0, 1)]
            new_top = jnp.maximum(top, jnp.maximum(parts[0][1], parts[1][1]))
            mine = jnp.exp(top - new_top)
            theirs = [jnp.exp(part[1] - new_top) for part in parts]
            total = total * mine + parts[0][2] * theirs[0] + parts[1][2] * theirs[1]
            share = float(width * NX * NY * NC) / total
            for j in range(STILES):
                cols = slice(j * TILE, (j + 1) * TILE)
                value = tiles[j] * mine
                for side in (0, 1):
                    code = in_code[side, 3, half, code_at, cols]
                    value = value + code.astype(F32) * (parts[side][0] * theirs[side])
                done_ref[row_at, cols] = value * share
    early = lax.broadcasted_iota(I32, (8, width), 0) < 4
    for p in range(4):
        second = pltpu.roll(done_ref[24 * p + 8 : 24 * p + 16, :], 4, 0)
        mixed = done_ref[24 * p + 16 : 24 * p + 24, :]
        out_ref[24 * p : 24 * p + 8, :] = done_ref[24 * p : 24 * p + 8, :]
        out_ref[24 * p + 8 : 24 * p + 16, :] = jnp.where(early, mixed, second)
        out_ref[24 * p + 16 : 24 * p + 24, :] = jnp.where(early, second, mixed)
    for copy in sent:
        copy.wait_send()


def exchange(slots, meta):
    width = STILES * TILE
    dma = pltpu.SemaphoreType.DMA
    return pl.pallas_call(
        exchange_kernel,
        out_shape=jax.ShapeDtypeStruct((96, width), F32),
        in_specs=[pl.BlockSpec(memory_space=pl.ANY)] * 2,
        out_specs=pl.BlockSpec(memory_space=pltpu.VMEM),
        scratch_shapes=[
            pltpu.VMEM((8, 8, CAP, 96, TILE), BF16),
            pltpu.VMEM((8, 32, 128), F32),
            pltpu.VMEM((8, 96, TILE), F32),
            pltpu.VMEM((16, 128), F32),
            pltpu.VMEM((96, width), F32),
            pltpu.VMEM((2, 4, 2, 48, width), I16),
            pltpu.VMEM((2, 4, 2, 48, width), I16),
            pltpu.VMEM((2, 4, 2, 16, 128), F32),
            pltpu.VMEM((2, 4, 2, 16, 128), F32),
            dma((8, 8)), dma((8, 8)), dma((8,)), dma((8,)),
            dma((2, 4, 2)), dma((2, 4, 2)), dma((2, 4, 2)), dma((2, 4, 2)),
        ],
        compiler_params=pltpu.CompilerParams(
            collective_id=1, has_side_effects=True, vmem_limit_bytes=VMEM_LIMIT
        ),
        name="exchange",
    )(slots, meta)


def per_device(hidden_states, head_weight, focus_tiles, focus_blocks):
    logits = gather_logits(hidden_states, head_weight)
    slots, meta = map_tiles(focus_tiles, logits, focus_blocks)
    return exchange(slots, meta)


def solution(mesh):
    return jax.shard_map(
        per_device,
        mesh=mesh,
        in_specs=(P("vocab", "hid"), P("hid", "vocab"), P("vocab", None), P("vocab", None, None)),
        out_specs=P("hid", "vocab"),
        check_vma=False,
    )
```
